256 devices in a mesh: group: 8 (over y, core), blk: 32 (over x, z).
Axes of the slice: x: 4, y: 4, z: 8, core: 2. Of those that a mesh axis runs over, the one named last changes fastest.
Arguments:
- sep_rhs: float32 [8, 4096, 256], P('group', 'blk'), may hold values from -6 to 6
- sep_inv: bfloat16 [8, 32, 128, 128], P('group', 'blk'), as said below
- fac_values: bfloat16 [8, 512, 128, 128], P('group', 'blk'), may hold values from -0.09375 to 0.09375
- fac_src: int32 [8, 512], P('group', 'blk'), may hold values from 0 to 31, as said below
- fac_count: int32 [8, 32], P('group', 'blk'), may hold values from 8 to 16, as said below
- sub_rhs: bfloat16 [8, 131072, 256], P('group', 'blk'), may hold values from -6 to 6
- sub_inv: bfloat16 [8, 1024, 128, 128], P('group', 'blk'), as said below
- sub_coup: bfloat16 [8, 1024, 128, 128], P('group', 'blk'), may hold values from -0.09375 to 0.09375
Outputs:
- sep_sol: bfloat16 [8, 4096, 256], P('group', 'blk')
- sub_sol: bfloat16 [8, 131072, 256], P('group', 'blk')
The draws below stay inside these ranges and needn't reach their ends.
Inputs may be any that keep to these rules, and one draw needn't show every extreme that they name: `fac_src`: each owner's 16 entries are distinct row blocks of the separator before. The first fac_count entries of an owner's slots are live; in every separator some owner has all 16 and some owner has 8. `sep_inv`: every block is lower triangular. `sub_inv`: every block is lower triangular.
All inputs are finite; a program needn't handle non-finite values.
Results may differ from the reference program's by a relative error of at most 0.015.
Values may be sent and summed in bfloat16 or wider, within the bound.
A program may use at most 64 MiB of HBM per device.

```python
import jax
import jax.numpy as jnp

COLUMNS = 256
BLOCK = 128
LOC_DEV = 32
GROUPS = 8
OWNERS = 32
FAC_DEV = 16


def lower_blocks(key, count):
    key_diag, key_off = jax.random.split(key)
    diag_vals = jax.random.uniform(key_diag, (count, BLOCK), jnp.float32, 0.5, 1.5)
    off_vals = jax.random.normal(key_off, (count, BLOCK, BLOCK), jnp.float32) * (0.6 * BLOCK ** (-0.5))
    row_ids = jnp.arange(BLOCK)[:, None]
    col_ids = jnp.arange(BLOCK)[None, :]
    lower_part = jnp.where(row_ids > col_ids, off_vals, 0.0)
    diag_part = jnp.where(row_ids == col_ids, diag_vals[:, :, None], 0.0)
    return lower_part + diag_part


def draw_sep_inv(key, part):
    return lower_blocks(key, GROUPS * OWNERS).reshape(GROUPS, OWNERS, BLOCK, BLOCK).astype(jnp.bfloat16)


def draw_sub_inv(key, part):
    return lower_blocks(key, GROUPS * OWNERS * LOC_DEV).reshape(GROUPS, OWNERS * LOC_DEV, BLOCK, BLOCK).astype(jnp.bfloat16)


def draw_fac_src(key, part):
    scores = jax.random.randint(key, (GROUPS, OWNERS, OWNERS), 0, 1 << 20) * OWNERS + jnp.arange(OWNERS, dtype=jnp.int32)
    ordered = jnp.argsort(scores, axis=-1, stable=True)
    return ordered[:, :, :FAC_DEV].reshape(GROUPS, OWNERS * FAC_DEV).astype(jnp.int32)


def draw_fac_count(key, part):
    key_base, key_busy = jax.random.split(key)
    base_count = jax.random.randint(key_base, (GROUPS, OWNERS), FAC_DEV // 2, FAC_DEV + 1)
    busy_owner = jax.random.randint(key_busy, (GROUPS, 1), 0, OWNERS)
    light_owner = (busy_owner + 1) % OWNERS
    owner_ids = jnp.arange(OWNERS, dtype=jnp.int32)[None, :]
    counts = jnp.where(owner_ids == light_owner, FAC_DEV // 2, base_count)
    return jnp.where(owner_ids == busy_owner, FAC_DEV, counts).astype(jnp.int32)


def block_levels(stream_key, extent, cuts, low, high):
    def one(dim, blocks):
        steps = jax.random.uniform(jax.random.fold_in(jax.random.fold_in(stream_key, 6), dim), (blocks,), jnp.float32, low / len(cuts), high / len(cuts))
        return jnp.repeat(jnp.exp(steps), extent[dim] // blocks).reshape((-1,) + (1,) * (len(extent) - dim - 1))

    factor_of = one(*cuts[0])
    for cut in cuts[1:]:
        factor_of = factor_of * one(*cut)
    return factor_of


def normal_values(stream_key, shape, spread, most, pieces=(), kind=jnp.bfloat16):
    array = spread * jax.random.normal(stream_key, shape, jnp.float32)
    if pieces:
        array = array * block_levels(stream_key, shape, pieces, -0.22, 0.18)
    return jnp.clip(array, -most, most).astype(kind)


def setup_inputs(seed: int = 0) -> dict:
    splits = jax.random.split(jax.random.key(seed), 9)
    sep_rhs = normal_values(splits[0], (GROUPS, OWNERS * BLOCK, COLUMNS), 1.0, 6.0, ((0, 8), (1, 32)), jnp.float32)
    sep_inv = draw_sep_inv(jax.random.fold_in(splits[8], 71), 0)
    fac_values = normal_values(splits[2], (GROUPS, OWNERS * FAC_DEV, BLOCK, BLOCK), (2 * BLOCK * FAC_DEV) ** -0.5, 0.09375, ((0, 8), (1, 32)))
    fac_src = draw_fac_src(jax.random.fold_in(splits[8], 71), 0)
    fac_count = draw_fac_count(jax.random.fold_in(splits[8], 71), 0)
    sub_rhs = normal_values(splits[5], (GROUPS, OWNERS * LOC_DEV * BLOCK, COLUMNS), 1.0, 6.0, ((0, 8), (1, 32)))
    sub_inv = draw_sub_inv(jax.random.fold_in(splits[8], 71), 0)
    sub_coup = normal_values(splits[7], (GROUPS, OWNERS * LOC_DEV, BLOCK, BLOCK), (BLOCK * LOC_DEV) ** -0.5, 0.09375, ((0, 8), (1, 32)))
    return {"sep_rhs": sep_rhs, "sep_inv": sep_inv, "fac_values": fac_values, "fac_src": fac_src, "fac_count": fac_count, "sub_rhs": sub_rhs, "sub_inv": sub_inv, "sub_coup": sub_coup}


def reference(sep_rhs, sep_inv, fac_values, fac_src, fac_count, sub_rhs, sub_inv, sub_coup):
    previous = jnp.zeros((OWNERS, BLOCK, COLUMNS), jnp.bfloat16)
    sep_parts = []
    sub_parts = []
    for group_pos in range(GROUPS):
        rhs_blocks = sub_rhs[group_pos].reshape(OWNERS * LOC_DEV, BLOCK, COLUMNS)
        local_sol = jnp.einsum("nab,nbr->nar", sub_inv[group_pos].astype(jnp.float32), rhs_blocks.astype(jnp.float32)).astype(jnp.bfloat16)
        lifted = jnp.einsum("olab,olbr->oar", sub_coup[group_pos].reshape(OWNERS, LOC_DEV, BLOCK, BLOCK).astype(jnp.float32), local_sol.reshape(OWNERS, LOC_DEV, BLOCK, COLUMNS).astype(jnp.float32))
        reduced = sep_rhs[group_pos].reshape(OWNERS, BLOCK, COLUMNS) - lifted
        source_ids = fac_src[group_pos].reshape(OWNERS, FAC_DEV)
        selected = previous[source_ids]
        slot_mask = (jnp.arange(FAC_DEV, dtype=jnp.int32)[None, :] < fac_count[group_pos][:, None]).astype(jnp.float32)
        selected = selected.astype(jnp.float32) * slot_mask[:, :, None, None]
        coupling = jnp.einsum("okab,okbr->oar", fac_values[group_pos].reshape(OWNERS, FAC_DEV, BLOCK, BLOCK).astype(jnp.float32), selected)
        corrected = (reduced - coupling).astype(jnp.bfloat16)
        solved = jnp.einsum("oab,obr->oar", sep_inv[group_pos].astype(jnp.float32), corrected.astype(jnp.float32)).astype(jnp.bfloat16)
        previous = solved
        sep_parts.append(solved.reshape(OWNERS * BLOCK, COLUMNS))
        sub_parts.append(local_sol.reshape(OWNERS * LOC_DEV * BLOCK, COLUMNS))
    return (jnp.stack(sep_parts), jnp.stack(sub_parts))
```

```python
import jax
import jax.numpy as jnp
from jax import lax
from jax.experimental import pallas as pl
from jax.experimental.pallas import tpu as pltpu
from jax.sharding import PartitionSpec as P

MESH = pl.DeviceIdType.MESH
F32, BF16, I32 = jnp.float32, jnp.bfloat16, jnp.int32

GROUPS = 8
CORES = 2
RINGS = GROUPS // CORES
XS, ZS = 4, 8
OWNERS = XS * ZS
BLOCK = 128
COLUMNS = 256
CHUNK = COLUMNS // GROUPS
HALVES = 2
HALF = CHUNK // HALVES
SLOTS = 16
SUBS = 32
LOADS = 8
PER = SUBS // LOADS

NT = (((1,), (1,)), ((), ()))


def ring(step, size):
    return min(step, size - step)


OFFSETS = sorted(
    ((dx, dz) for dx in range(XS) for dz in range(ZS) if (dx, dz) != (0, 0)),
    key=lambda p: -(ring(p[0], XS) + ring(p[1], ZS)),
)


def kernel(
    sep_rhs, sep_inv, fac, src, count, sub_rhs, sub_inv, sub_coup,
    sep_out, sub_out,
    rhs_v, inv_v, coup_v, sol_v, sep_v, red_t, red_all, low_all, fac_all,
    src_v, count_s, idx_v, idx_s, home, result,
    *rest,
):
    gath = [rest[t * HALVES : (t + 1) * HALVES] for t in range(GROUPS)]
    (
        load_sem, small_sem, sub_sem, red_send, red_sem, low_send, low_sem, fac_send, fac_fwd, fac_sem,
        idx_send, idx_sem, idx_local, x_send, x_sem, home_send, home_sem, out_sem,
    ) = rest[GROUPS * HALVES :]
    g, o = lax.axis_index("group"), lax.axis_index("blk")
    y, core = g // CORES, lax.rem(g, CORES)
    x, z = o // ZS, lax.rem(o, ZS)

    def owner(dx, dz):
        return {"blk": lax.rem(x + dx, XS) * ZS + lax.rem(z + dz, ZS)}

    def group_peer(d):
        return {"group": lax.rem(g + d, GROUPS)}

    def y_peer(d):
        return {"group": lax.rem(y + d, RINGS) * CORES + core}

    sibling = {"group": y * CORES + 1 - core}

    def remote(source, target, send, recv, device):
        return pltpu.make_async_remote_copy(
            src_ref=source, dst_ref=target, send_sem=send, recv_sem=recv,
            device_id=device, device_id_type=MESH,
        )

    def drain(ref, sem):
        pltpu.make_async_copy(ref, ref, sem).wait()

    rows = PER * BLOCK

    def loads(c):
        part, blocks = pl.ds(c * rows, rows), pl.ds(c * PER, PER)
        return (
            pltpu.make_async_copy(sub_rhs.at[0, part], rhs_v.at[part], load_sem.at[0, c]),
            pltpu.make_async_copy(sub_inv.at[0, blocks], inv_v.at[blocks], load_sem.at[1, c]),
            pltpu.make_async_copy(sub_coup.at[0, blocks], coup_v.at[blocks], load_sem.at[2, c]),
        )

    for c in range(LOADS):
        for copy in loads(c):
            copy.start()
    small = (
        pltpu.make_async_copy(sep_rhs.at[0], sep_v, small_sem.at[0]),
        pltpu.make_async_copy(src, src_v, small_sem.at[1]),
        pltpu.make_async_copy(count, count_s, small_sem.at[2]),
    )
    for copy in small:
        copy.start()
    pltpu.make_async_copy(sep_inv.at[0, 0], low_all.at[g], low_sem.at[g]).start()
    pltpu.make_async_copy(fac.at[0], fac_all.at[g], fac_sem.at[g]).start()

    barrier = pltpu.get_barrier_semaphore()
    for dx, dz in OFFSETS:
        pl.semaphore_signal(barrier, inc=1, device_id=owner(dx, dz), device_id_type=MESH)
    for d in range(1, GROUPS):
        pl.semaphore_signal(barrier, inc=1, device_id=group_peer(d), device_id_type=MESH)

    for t in range(GROUPS - 1):
        for h in range(HALVES):
            gath[t][h][OWNERS] = jnp.zeros((HALF, BLOCK), BF16)
    for copy in small:
        copy.wait()
    slot = lax.broadcasted_iota(I32, (1, SLOTS), 1)
    idx_v[g] = jnp.zeros((1, BLOCK), I32)
    idx_v[g, :, pl.ds(0, SLOTS)] = jnp.where(slot < count_s[0, 0], src_v[...], OWNERS)

    def subtree(c, total):
        for copy in loads(c):
            copy.wait()
        solved = []
        for i in range(PER):
            n = c * PER + i
            part = pl.ds(pl.multiple_of(n * BLOCK, BLOCK), BLOCK)
            sol = jnp.dot(inv_v[n], rhs_v[part, :], preferred_element_type=F32).astype(BF16)
            sol_v[part, :] = sol
            solved.append(sol)
        part = pl.ds(pl.multiple_of(c * rows, rows), rows)
        pltpu.make_async_copy(sol_v.at[part], sub_out.at[0, part], sub_sem.at[c]).start()
        coup = jnp.concatenate([coup_v[c * PER + i] for i in range(PER)], axis=1)
        return total + jnp.dot(coup, jnp.concatenate(solved, axis=0), preferred_element_type=F32)

    lifted = lax.fori_loop(0, LOADS, subtree, jnp.zeros((BLOCK, COLUMNS), F32))
    red_t[...] = jnp.transpose(sep_v[...] - lifted).reshape(GROUPS, CHUNK, BLOCK)

    pl.semaphore_wait(barrier, len(OFFSETS) + GROUPS - 1)

    pltpu.make_async_copy(red_t.at[g], red_all.at[g], red_sem.at[g]).start()
    for d in (4, 5, 3, 6, 2, 7, 1):
        peer = group_peer(d)
        remote(red_t.at[peer["group"]], red_all.at[g], red_send, red_sem.at[g], peer).start()
        remote(sep_inv.at[0, 0], low_all.at[g], low_send, low_sem.at[g], peer).start()
    for d in range(1, GROUPS):
        remote(idx_v.at[g], idx_v.at[g], idx_send, idx_sem.at[g], group_peer(d)).start()

    def send_factors():
        for d in (2, 1, 3):
            remote(fac.at[0], fac_all.at[g], fac_send.at[d], fac_sem.at[g], y_peer(d)).start()
        remote(fac.at[0], fac_all.at[g], fac_send.at[0], fac_sem.at[g], sibling).start()

    early = 4

    @pl.when((g >= 1) & (g < early))
    def _():
        send_factors()

    def forwards(t):
        return (core == t % CORES) & (y != t // CORES)

    def pass_on(t):
        @pl.when(forwards(t))
        def _():
            drain(fac_all.at[t], fac_sem.at[t])
            remote(fac_all.at[t], fac_all.at[t], fac_fwd.at[t], fac_sem.at[t], sibling).start()

    drain(red_all.at[0], red_sem.at[0])
    drain(low_all.at[0], low_sem.at[0])
    for t in range(GROUPS):
        if t == 1:
            for other in range(GROUPS):
                @pl.when(g != other)
                def _():
                    drain(idx_v.at[other], idx_sem.at[other])
            copy = pltpu.make_async_copy(idx_v, idx_s, idx_local)
            copy.start()
            copy.wait()
        if t:
            drain(red_all.at[t], red_sem.at[t])
            drain(low_all.at[t], low_sem.at[t])

            @pl.when(jnp.logical_not(forwards(t)))
            def _():
                drain(fac_all.at[t], fac_sem.at[t])

        for h in range(HALVES):
            target = red_all[t, pl.ds(h * HALF, HALF), :]
            if t:
                before = gath[t - 1][h]
                drain(before.at[pl.ds(0, OWNERS - 1)], x_sem.at[t - 1, h])
                chosen = jnp.concatenate([before[idx_s[t, 0, k]] for k in range(SLOTS)], axis=1)
                factors = jnp.concatenate([fac_all[t, k] for k in range(SLOTS)], axis=1)
                target = target - lax.dot_general(chosen, factors, NT, preferred_element_type=F32)
            solved = lax.dot_general(
                target.astype(BF16), low_all[t], NT, preferred_element_type=F32
            ).astype(BF16)
            mine = gath[t][h]
            mine[o] = solved
            if t < GROUPS - 1:
                for dx, dz in OFFSETS:
                    remote(
                        mine.at[o], mine.at[o], x_send.at[t, h], x_sem.at[t, h], owner(dx, dz)
                    ).start()

            @pl.when(g == t)
            def _():
                pltpu.make_async_copy(mine.at[o], home.at[g, h], home_sem).start()

            @pl.when(g != t)
            def _():
                remote(
                    mine.at[o], home.at[g, h], home_send.at[t, h], home_sem, {"group": t}
                ).start()

        if t == 0:
            @pl.when(g >= early)
            def _():
                send_factors()
        if t < GROUPS - 1:
            pass_on(t + 1)

    drain(home, home_sem)
    whole = home[...].reshape(COLUMNS, BLOCK).astype(F32)
    result[...] = jnp.transpose(whole).astype(BF16)
    out = pltpu.make_async_copy(result, sep_out.at[0], out_sem)
    out.start()

    for c in range(LOADS):
        part = pl.ds(c * rows, rows)
        pltpu.make_async_copy(sol_v.at[part], sub_out.at[0, part], sub_sem.at[c]).wait()
    drain(red_t.at[pl.ds(0, GROUPS - 1)], red_send)
    drain(low_all.at[pl.ds(0, GROUPS - 1)], low_send)
    drain(idx_v.at[pl.ds(0, GROUPS - 1)], idx_send)

    @pl.when(g >= 1)
    def _():
        for d in range(RINGS):
            drain(fac_all.at[0], fac_send.at[d])

    @pl.when(g == 0)
    def _():
        drain(fac_all.at[0], fac_sem.at[0])

    for t in range(1, GROUPS):
        @pl.when(forwards(t))
        def _():
            drain(fac_all.at[t], fac_fwd.at[t])
    for t in range(GROUPS):
        for h in range(HALVES):
            if t < GROUPS - 1:
                drain(gath[t][h].at[pl.ds(0, OWNERS - 1)], x_send.at[t, h])

            @pl.when(g != t)
            def _():
                drain(gath[t][h].at[0], home_send.at[t, h])
    out.wait()


def on_device(*args):
    dma = pltpu.SemaphoreType.DMA
    scratch = [
        pltpu.VMEM((SUBS * BLOCK, COLUMNS), BF16),
        pltpu.VMEM((SUBS, BLOCK, BLOCK), BF16),
        pltpu.VMEM((SUBS, BLOCK, BLOCK), BF16),
        pltpu.VMEM((SUBS * BLOCK, COLUMNS), BF16),
        pltpu.VMEM((BLOCK, COLUMNS), F32),
        pltpu.VMEM((GROUPS, CHUNK, BLOCK), F32),
        pltpu.VMEM((GROUPS, CHUNK, BLOCK), F32),
        pltpu.VMEM((GROUPS, BLOCK, BLOCK), BF16),
        pltpu.VMEM((GROUPS, SLOTS, BLOCK, BLOCK), BF16),
        pltpu.VMEM((1, SLOTS), I32),
        pltpu.SMEM((1, 1), I32),
        pltpu.VMEM((GROUPS, 1, BLOCK), I32),
        pltpu.SMEM((GROUPS, 1, BLOCK), I32),
        pltpu.VMEM((GROUPS, HALVES, HALF, BLOCK), BF16),
        pltpu.VMEM((BLOCK, COLUMNS), BF16),
        *[pltpu.VMEM((OWNERS + 1, HALF, BLOCK), BF16)] * (GROUPS * HALVES),
        dma((3, LOADS)), dma((3,)), dma((LOADS,)),
        dma, dma((GROUPS,)), dma, dma((GROUPS,)),
        dma((RINGS,)), dma((GROUPS,)), dma((GROUPS,)),
        dma, dma((GROUPS,)), dma,
        dma((GROUPS, HALVES)), dma((GROUPS, HALVES)), dma((GROUPS, HALVES)), dma, dma,
    ]
    return pl.pallas_call(
        kernel,
        out_shape=(
            jax.ShapeDtypeStruct((1, BLOCK, COLUMNS), BF16),
            jax.ShapeDtypeStruct((1, SUBS * BLOCK, COLUMNS), BF16),
        ),
        in_specs=[pl.BlockSpec(memory_space=pl.ANY)] * 8,
        out_specs=[pl.BlockSpec(memory_space=pl.ANY)] * 2,
        scratch_shapes=scratch,
        compiler_params=pltpu.CompilerParams(
            collective_id=0, has_side_effects=True, vmem_limit_bytes=48 << 20
        ),
    )(*args)


def solution(mesh):
    rows = P("group", "blk", None)
    blocks = P("group", "blk", None, None)
    flat = P("group", "blk")
    return jax.shard_map(
        on_device,
        mesh=mesh,
        in_specs=(rows, blocks, blocks, flat, flat, rows, blocks, blocks),
        out_specs=(rows, rows),
        check_vma=False,
    )
```

```python
import jax
import jax.numpy as jnp
from jax import lax
from jax.experimental import pallas as pl
from jax.experimental.pallas import tpu as pltpu
from jax.sharding import PartitionSpec as P

MESH = pl.DeviceIdType.MESH
F32, BF16, I32 = jnp.float32, jnp.bfloat16, jnp.int32

GROUPS = 8
CORES = 2
RINGS = GROUPS // CORES
XS, ZS = 4, 8
OWNERS = XS * ZS
BLOCK = 128
COLUMNS = 256
CHUNK = COLUMNS // GROUPS
HALVES = 2
HALF = CHUNK // HALVES
SLOTS = 16
SUBS = 32
LOADS = 8
PER = SUBS // LOADS

PARTS = ((0, SLOTS // 2), (SLOTS // 2, SLOTS // 2))

NT = (((1,), (1,)), ((), ()))


def ring(step, size):
    return min(step, size - step)


OFFSETS = sorted(
    ((dx, dz) for dx in range(XS) for dz in range(ZS) if (dx, dz) != (0, 0)),
    key=lambda p: -(ring(p[0], XS) + ring(p[1], ZS)),
)


def kernel(
    sep_rhs, sep_inv, fac, src, count, sub_rhs, sub_inv, sub_coup,
    sep_out, sub_out,
    rhs_v, inv_v, coup_v, sol_v, sep_v, low_v, first_t, red_t, red_all, fac_all,
    src_v, count_s, idx_v, idx_s, home, result,
    *rest,
):
    gath = [rest[t * HALVES : (t + 1) * HALVES] for t in range(GROUPS)]
    (
        load_sem, small_sem, sub_sem, first_send, first_sem, red_send, red_sem, fac_send, fac_fwd, fac_sem,
        idx_send, idx_sem, idx_local, x_send, x_sem, home_send, home_sem, out_sem,
    ) = rest[GROUPS * HALVES :]
    g, o = lax.axis_index("group"), lax.axis_index("blk")
    y, core = g // CORES, lax.rem(g, CORES)
    x, z = o // ZS, lax.rem(o, ZS)

    def owner(dx, dz):
        return {"blk": lax.rem(x + dx, XS) * ZS + lax.rem(z + dz, ZS)}

    def group_peer(d):
        return {"group": lax.rem(g + d, GROUPS)}

    def y_peer(d):
        return {"group": lax.rem(y + d, RINGS) * CORES + core}

    sibling = {"group": y * CORES + 1 - core}

    def remote(source, target, send, recv, device):
        return pltpu.make_async_remote_copy(
            src_ref=source, dst_ref=target, send_sem=send, recv_sem=recv,
            device_id=device, device_id_type=MESH,
        )

    def drain(ref, sem):
        pltpu.make_async_copy(ref, ref, sem).wait()

    barrier = pltpu.get_barrier_semaphore()
    for dx, dz in OFFSETS:
        pl.semaphore_signal(barrier, inc=1, device_id=owner(dx, dz), device_id_type=MESH)
    for d in range(1, GROUPS):
        pl.semaphore_signal(barrier, inc=1, device_id=group_peer(d), device_id_type=MESH)

    rows = PER * BLOCK

    def loads(c):
        part, blocks = pl.ds(c * rows, rows), pl.ds(c * PER, PER)
        return (
            pltpu.make_async_copy(sub_rhs.at[0, part], rhs_v.at[part], load_sem.at[0, c]),
            pltpu.make_async_copy(sub_inv.at[0, blocks], inv_v.at[blocks], load_sem.at[1, c]),
            pltpu.make_async_copy(sub_coup.at[0, blocks], coup_v.at[blocks], load_sem.at[2, c]),
        )

    for c in range(LOADS):
        for copy in loads(c):
            copy.start()
    small = (
        pltpu.make_async_copy(sep_rhs.at[0], sep_v, small_sem.at[0]),
        pltpu.make_async_copy(src, src_v, small_sem.at[1]),
        pltpu.make_async_copy(count, count_s, small_sem.at[2]),
        pltpu.make_async_copy(sep_inv.at[0, 0], low_v, small_sem.at[3]),
    )
    for copy in small:
        copy.start()
    def pieces(p):
        first, size = PARTS[p]
        some = pl.ds(first, size)
        two = [(fac.at[0, some], fac_all.at[g, some])]
        return two + [(sep_inv.at[0, 0], fac_all.at[g, SLOTS])] * p

    def fac_part(t, p):
        first, size = PARTS[p]
        return fac_all.at[t, pl.ds(first, size + p)]

    for p in range(2):
        for source, target in pieces(p):
            pltpu.make_async_copy(source, target, fac_sem.at[p, g]).start()

    for t in range(GROUPS - 1):
        for h in range(HALVES):
            gath[t][h][OWNERS] = jnp.zeros((HALF, BLOCK), BF16)
    for copy in small:
        copy.wait()
    slot = lax.broadcasted_iota(I32, (1, SLOTS), 1)
    idx_v[0] = jnp.zeros((1, BLOCK), I32)
    idx_v[g] = jnp.zeros((1, BLOCK), I32)
    idx_v[g, :, pl.ds(0, SLOTS)] = jnp.where(slot < count_s[0, 0], src_v[...], OWNERS)

    def subtree(c, total):
        for copy in loads(c):
            copy.wait()
        solved = []
        for i in range(PER):
            n = c * PER + i
            part = pl.ds(pl.multiple_of(n * BLOCK, BLOCK), BLOCK)
            sol = jnp.dot(inv_v[n], rhs_v[part, :], preferred_element_type=F32).astype(BF16)
            sol_v[part, :] = sol
            solved.append(sol)
        part = pl.ds(pl.multiple_of(c * rows, rows), rows)
        pltpu.make_async_copy(sol_v.at[part], sub_out.at[0, part], sub_sem.at[c]).start()
        coup = jnp.concatenate([coup_v[c * PER + i] for i in range(PER)], axis=1)
        return total + jnp.dot(coup, jnp.concatenate(solved, axis=0), preferred_element_type=F32)

    lifted = lax.fori_loop(0, LOADS, subtree, jnp.zeros((BLOCK, COLUMNS), F32))
    reduced = sep_v[...] - lifted
    red_t[...] = jnp.transpose(reduced).reshape(GROUPS, CHUNK, BLOCK)
    @pl.when(g == 0)
    def _():
        first = jnp.dot(low_v[...], reduced.astype(BF16), preferred_element_type=F32)
        first_t[...] = jnp.transpose(first).astype(BF16).reshape(GROUPS, HALVES, HALF, BLOCK)
        result[...] = first.astype(BF16)

    pl.semaphore_wait(barrier, len(OFFSETS) + GROUPS - 1)

    @pl.when(g == 0)
    def _():
        for h in range(HALVES):
            for d in (4, 5, 3, 2, 6, 7, 1):
                remote(
                    first_t.at[d, h], gath[0][h].at[o], first_send, first_sem.at[h], {"group": d}
                ).start()
            pltpu.make_async_copy(first_t.at[0, h], gath[0][h].at[o], first_sem.at[h]).start()

    def send_reduced():
        pltpu.make_async_copy(red_t.at[g], red_all.at[g], red_sem.at[g]).start()
        for d in (4, 5, 3, 6, 2, 7, 1):
            peer = group_peer(d)
            remote(red_t.at[peer["group"]], red_all.at[g], red_send, red_sem.at[g], peer).start()

    def send_factors():
        def to(d, p):
            for source, target in pieces(p):
                peer = y_peer(d) if d else sibling
                remote(source, target, fac_send.at[p, d], fac_sem.at[p, g], peer).start()

        to(3, 1)
        to(1, 1)

        @pl.when(g == 1)
        def _():
            to(2, 0)

        to(3, 0)
        to(1, 0)
        to(0, 1)
        to(0, 0)

    def send_indices():
        for d in range(1, GROUPS):
            remote(idx_v.at[g], idx_v.at[g], idx_send, idx_sem.at[g], group_peer(d)).start()

    def send_ahead(t):
        @pl.when(g == t)
        def _():
            send_reduced()

        if t == 1:
            @pl.when(g >= 1)
            def _():
                send_indices()

    def send_factors_of(t, until):
        @pl.when((g >= t) & (g < until))
        def _():
            send_factors()

    def forwards(t):
        return (core == t % CORES) & (y != t // CORES)

    def relays(t):
        return (core == t % CORES) & (y == (t // CORES - 1) % RINGS)

    def relayed(t):
        return (1,) if t == 1 else (1, 0)

    def forward(t, relay):
        for p in (1, 0):
            drain(fac_part(t, p), fac_sem.at[p, t])
            if relay and p in relayed(t):
                remote(
                    fac_part(t, p), fac_part(t, p), fac_fwd.at[1, p, t], fac_sem.at[p, t], y_peer(RINGS - 1)
                ).start()
            remote(fac_part(t, p), fac_part(t, p), fac_fwd.at[0, p, t], fac_sem.at[p, t], sibling).start()

    def pass_on(step):
        for t in range(1, GROUPS):
            if max(0, t - 2) == step:
                @pl.when(relays(t))
                def _():
                    forward(t, True)

        if step + 1 < GROUPS:
            @pl.when(forwards(step + 1) & jnp.logical_not(relays(step + 1)))
            def _():
                forward(step + 1, False)

    send_ahead(1)
    send_ahead(2)
    send_factors_of(1, 3)

    def spread(t, h):
        mine = gath[t][h]
        for dx, dz in OFFSETS:
            remote(mine.at[o], mine.at[o], x_send.at[t, h], x_sem.at[t, h], owner(dx, dz)).start()

    for t in range(GROUPS):
        if t == 1:
            for other in range(1, GROUPS):
                @pl.when(g != other)
                def _():
                    drain(idx_v.at[other], idx_sem.at[other])
            copy = pltpu.make_async_copy(idx_v, idx_s, idx_local)
            copy.start()
            copy.wait()
        if t:
            drain(red_all.at[t], red_sem.at[t])

            @pl.when(jnp.logical_not(forwards(t)))
            def _():
                for p in range(2):
                    drain(fac_part(t, p), fac_sem.at[p, t])

        for h in range(HALVES):
            mine = gath[t][h]
            if t == 0:
                drain(mine.at[o], first_sem.at[h])
                spread(t, h)
                continue
            before = gath[t - 1][h]
            drain(before.at[pl.ds(0, OWNERS - 1)], x_sem.at[t - 1, h])
            chosen = jnp.concatenate([before[idx_s[t, 0, k]] for k in range(SLOTS)], axis=1)
            factors = jnp.concatenate([fac_all[t, k] for k in range(SLOTS)], axis=1)
            coupling = lax.dot_general(chosen, factors, NT, preferred_element_type=F32)
            corrected = (red_all[t, pl.ds(h * HALF, HALF), :] - coupling).astype(BF16)
            solved = lax.dot_general(corrected, fac_all[t, SLOTS], NT, preferred_element_type=F32)
            mine[o] = solved.astype(BF16)
            if t < GROUPS - 1:
                spread(t, h)

            @pl.when(g == t)
            def _():
                pltpu.make_async_copy(mine.at[o], home.at[g, h], home_sem).start()

            @pl.when(g != t)
            def _():
                remote(
                    mine.at[o], home.at[g, h], home_send.at[t, h], home_sem, {"group": t}
                ).start()

        if t + 3 < GROUPS:
            send_ahead(t + 3)
            send_factors_of(t + 3, t + 4)
        if t < GROUPS - 1:
            pass_on(t)

    @pl.when(g >= 1)
    def _():
        drain(home, home_sem)
        whole = home[...].reshape(COLUMNS, BLOCK).astype(F32)
        result[...] = jnp.transpose(whole).astype(BF16)

    out = pltpu.make_async_copy(result, sep_out.at[0], out_sem)
    out.start()

    for c in range(LOADS):
        part = pl.ds(c * rows, rows)
        pltpu.make_async_copy(sol_v.at[part], sub_out.at[0, part], sub_sem.at[c]).wait()

    @pl.when(g >= 1)
    def _():
        drain(red_t.at[pl.ds(0, GROUPS - 1)], red_send)
        drain(idx_v.at[pl.ds(0, GROUPS - 1)], idx_send)
        for d in (0, 1, 3):
            for p in range(2):
                drain(fac_part(0, p), fac_send.at[p, d])

    @pl.when(g == 1)
    def _():
        drain(fac_part(0, 0), fac_send.at[0, 2])

    @pl.when(g == 0)
    def _():
        drain(first_t.at[pl.ds(0, GROUPS - 1)], first_send)
        for p in range(2):
            drain(fac_part(0, p), fac_sem.at[p, 0])

    for t in range(1, GROUPS):
        @pl.when(forwards(t))
        def _():
            for p in range(2):
                drain(fac_part(t, p), fac_fwd.at[0, p, t])

        @pl.when(relays(t))
        def _():
            for p in relayed(t):
                drain(fac_part(t, p), fac_fwd.at[1, p, t])

    for t in range(GROUPS):
        for h in range(HALVES):
            if t < GROUPS - 1:
                drain(gath[t][h].at[pl.ds(0, OWNERS - 1)], x_send.at[t, h])
            if t:
                @pl.when(g != t)
                def _():
                    drain(gath[t][h].at[0], home_send.at[t, h])
    out.wait()


def on_device(*args):
    dma = pltpu.SemaphoreType.DMA
    scratch = [
        pltpu.VMEM((SUBS * BLOCK, COLUMNS), BF16),
        pltpu.VMEM((SUBS, BLOCK, BLOCK), BF16),
        pltpu.VMEM((SUBS, BLOCK, BLOCK), BF16),
        pltpu.VMEM((SUBS * BLOCK, COLUMNS), BF16),
        pltpu.VMEM((BLOCK, COLUMNS), F32),
        pltpu.VMEM((BLOCK, BLOCK), BF16),
        pltpu.VMEM((GROUPS, HALVES, HALF, BLOCK), BF16),
        pltpu.VMEM((GROUPS, CHUNK, BLOCK), F32),
        pltpu.VMEM((GROUPS, CHUNK, BLOCK), F32),
        pltpu.VMEM((GROUPS, SLOTS + 1, BLOCK, BLOCK), BF16),
        pltpu.VMEM((1, SLOTS), I32),
        pltpu.SMEM((1, 1), I32),
        pltpu.VMEM((GROUPS, 1, BLOCK), I32),
        pltpu.SMEM((GROUPS, 1, BLOCK), I32),
        pltpu.VMEM((GROUPS, HALVES, HALF, BLOCK), BF16),
        pltpu.VMEM((BLOCK, COLUMNS), BF16),
        *[pltpu.VMEM((OWNERS + 1, HALF, BLOCK), BF16)] * (GROUPS * HALVES),
        dma((3, LOADS)), dma((4,)), dma((LOADS,)),
        dma, dma((HALVES,)), dma, dma((GROUPS,)),
        dma((2, RINGS)), dma((2, 2, GROUPS)), dma((2, GROUPS)),
        dma, dma((GROUPS,)), dma,
        dma((GROUPS, HALVES)), dma((GROUPS, HALVES)), dma((GROUPS, HALVES)), dma, dma,
    ]
    return pl.pallas_call(
        kernel,
        out_shape=(
            jax.ShapeDtypeStruct((1, BLOCK, COLUMNS), BF16),
            jax.ShapeDtypeStruct((1, SUBS * BLOCK, COLUMNS), BF16),
        ),
        in_specs=[pl.BlockSpec(memory_space=pl.ANY)] * 8,
        out_specs=[pl.BlockSpec(memory_space=pl.ANY)] * 2,
        scratch_shapes=scratch,
        compiler_params=pltpu.CompilerParams(
            collective_id=0, has_side_effects=True, vmem_limit_bytes=48 << 20
        ),
    )(*[a if i == 4 else pltpu.with_memory_space_constraint(a, pltpu.HBM) for i, a in enumerate(args)])


def solution(mesh):
    rows = P("group", "blk", None)
    blocks = P("group", "blk", None, None)
    flat = P("group", "blk")
    return jax.shard_map(
        on_device,
        mesh=mesh,
        in_specs=(rows, blocks, blocks, flat, flat, rows, blocks, blocks),
        out_specs=(rows, rows),
        check_vma=False,
    )
```

```python
import jax
import jax.numpy as jnp
from jax import lax
from jax.experimental import pallas as pl
from jax.experimental.pallas import tpu as pltpu
from jax.sharding import PartitionSpec as P

MESH = pl.DeviceIdType.MESH
F32, BF16, I32 = jnp.float32, jnp.bfloat16, jnp.int32

GROUPS = 8
CORES = 2
RINGS = GROUPS // CORES
XS, ZS = 4, 8
OWNERS = XS * ZS
BLOCK = 128
COLUMNS = 256
CHUNK = COLUMNS // GROUPS
HALVES = 2
HALF = CHUNK // HALVES
SLOTS = 16
SUBS = 32
LOADS = 4
PER = SUBS // LOADS
MEET_AT = 2

PARTS = ((0, SLOTS // 2), (SLOTS // 2, SLOTS // 2))

NT = (((1,), (1,)), ((), ()))


def ring(step, size):
    return min(step, size - step)


OFFSETS = sorted(
    ((dx, dz) for dx in range(XS) for dz in range(ZS) if (dx, dz) != (0, 0)),
    key=lambda p: -(ring(p[0], XS) + ring(p[1], ZS)),
)


def kernel(
    sep_rhs, sep_inv, fac, src, count, sub_rhs, sub_inv, sub_coup,
    sep_out, sub_out,
    rhs_v, inv_v, coup_v, sol_v, sep_v, low_v, first_t, red_t, red_all, fac_all,
    src_v, count_s, idx_v, idx_s, home,
    *rest,
):
    gath = [rest[t * HALVES : (t + 1) * HALVES] for t in range(GROUPS)]
    (
        load_sem, small_sem, sub_sem, first_send, first_sem, red_send, red_sem, fac_send, fac_fwd, fac_sem,
        idx_send, idx_sem, idx_local, x_send, x_sem, home_send, home_sem,
    ) = rest[GROUPS * HALVES :]
    g, o = lax.axis_index("group"), lax.axis_index("blk")
    y, core = g // CORES, lax.rem(g, CORES)
    x, z = o // ZS, lax.rem(o, ZS)

    def owner(dx, dz):
        return {"blk": lax.rem(x + dx, XS) * ZS + lax.rem(z + dz, ZS)}

    def group_peer(d):
        return {"group": lax.rem(g + d, GROUPS)}

    def y_peer(d):
        return {"group": lax.rem(y + d, RINGS) * CORES + core}

    sibling = {"group": y * CORES + 1 - core}

    def remote(source, target, send, recv, device):
        return pltpu.make_async_remote_copy(
            src_ref=source, dst_ref=target, send_sem=send, recv_sem=recv,
            device_id=device, device_id_type=MESH,
        )

    def drain(ref, sem):
        pltpu.make_async_copy(ref, ref, sem).wait()

    barrier = pltpu.get_barrier_semaphore()
    for dx, dz in OFFSETS:
        pl.semaphore_signal(barrier, inc=1, device_id=owner(dx, dz), device_id_type=MESH)
    for d in range(1, GROUPS):
        pl.semaphore_signal(barrier, inc=1, device_id=group_peer(d), device_id_type=MESH)

    rows = PER * BLOCK

    def loads(c):
        part, blocks = pl.ds(c * rows, rows), pl.ds(c * PER, PER)
        return (
            pltpu.make_async_copy(sub_rhs.at[0, part], rhs_v.at[part], load_sem.at[0, c]),
            pltpu.make_async_copy(sub_inv.at[0, blocks], inv_v.at[blocks], load_sem.at[1, c]),
            pltpu.make_async_copy(sub_coup.at[0, blocks], coup_v.at[blocks], load_sem.at[2, c]),
        )

    for c in range(LOADS):
        for copy in loads(c):
            copy.start()
    small = (
        pltpu.make_async_copy(sep_rhs.at[0], sep_v, small_sem.at[0]),
        pltpu.make_async_copy(src, src_v, small_sem.at[1]),
        pltpu.make_async_copy(count, count_s, small_sem.at[2]),
        pltpu.make_async_copy(sep_inv.at[0, 0], low_v, small_sem.at[3]),
    )
    for copy in small:
        copy.start()
    def pieces(p):
        first, size = PARTS[p]
        some = pl.ds(first, size)
        two = [(fac.at[0, some], fac_all.at[g, some])]
        return two + [(sep_inv.at[0, 0], fac_all.at[g, SLOTS])] * p

    def fac_part(t, p):
        first, size = PARTS[p]
        return fac_all.at[t, pl.ds(first, size + p)]

    for p in range(2):
        for source, target in pieces(p):
            pltpu.make_async_copy(source, target, fac_sem.at[p, g]).start()

    for t in range(GROUPS - 1):
        for h in range(HALVES):
            gath[t][h][OWNERS] = jnp.zeros((HALF, BLOCK), BF16)
    for copy in small:
        copy.wait()
    slot = lax.broadcasted_iota(I32, (1, SLOTS), 1)
    idx_v[0] = jnp.zeros((1, BLOCK), I32)
    idx_v[g] = jnp.zeros((1, BLOCK), I32)
    idx_v[g, :, pl.ds(0, SLOTS)] = jnp.where(slot < count_s[0, 0], src_v[...], OWNERS)

    def send_factors(parts=(1, 0)):
        def to(d, p):
            for source, target in pieces(p):
                peer = y_peer(d) if d else sibling
                remote(source, target, fac_send.at[p, d], fac_sem.at[p, g], peer).start()

        if 1 in parts:
            to(3, 1)
            to(1, 1)

        if 0 in parts:
            @pl.when(g == 1)
            def _():
                to(2, 0)

            to(3, 0)
            to(1, 0)
            to(0, 1)
            to(0, 0)

    def send_factors_of(t, until, parts=(1, 0)):
        @pl.when((g >= t) & (g < until))
        def _():
            send_factors(parts)

    def send_indices():
        for d in range(1, GROUPS):
            remote(idx_v.at[g], idx_v.at[g], idx_send, idx_sem.at[g], group_peer(d)).start()

    def solve(c):
        for copy in loads(c):
            copy.wait()
        for i in range(PER):
            n = c * PER + i
            own = pl.ds(pl.multiple_of(n * BLOCK, BLOCK), BLOCK)
            sol = jnp.dot(inv_v[n], rhs_v[own, :], preferred_element_type=F32)
            sol_v[own, :] = sol.astype(BF16)
        part = pl.ds(pl.multiple_of(c * rows, rows), rows)
        pltpu.make_async_copy(sol_v.at[part], sub_out.at[0, part], sub_sem.at[c]).start()

    def lift(c, total):
        part = pl.ds(pl.multiple_of(c * rows, rows), rows)
        coup = jnp.concatenate([coup_v[c * PER + i] for i in range(PER)], axis=1)
        return total + jnp.dot(coup, sol_v[part, :], preferred_element_type=F32)

    def subtree(c, total):
        total = lift(c - 1, total)
        solve(c)
        return total

    solve(0)
    lifted = lax.fori_loop(1, MEET_AT, subtree, jnp.zeros((BLOCK, COLUMNS), F32))

    pl.semaphore_wait(barrier, len(OFFSETS) + GROUPS - 1)
    @pl.when(g >= 1)
    def _():
        send_indices()

    send_factors_of(1, 3, (1,))

    lifted = lax.fori_loop(MEET_AT, LOADS, subtree, lifted)
    lifted = lift(LOADS - 1, lifted)
    reduced = sep_v[...] - lifted
    red_t[...] = jnp.transpose(reduced).reshape(GROUPS, CHUNK, BLOCK)
    @pl.when(g == 0)
    def _():
        first = jnp.dot(low_v[...], reduced.astype(BF16), preferred_element_type=F32)
        first_t[...] = jnp.transpose(first).astype(BF16).reshape(GROUPS, HALVES, HALF, BLOCK)
        sep_out[0] = first.astype(BF16)

    @pl.when(g == 0)
    def _():
        for h in range(HALVES):
            for d in (4, 5, 3, 2, 6, 7, 1):
                remote(
                    first_t.at[d, h], gath[0][h].at[o], first_send, first_sem.at[h], {"group": d}
                ).start()
            pltpu.make_async_copy(first_t.at[0, h], gath[0][h].at[o], first_sem.at[h]).start()

    def send_reduced():
        pltpu.make_async_copy(red_t.at[g], red_all.at[g], red_sem.at[g]).start()
        for d in (4, 5, 3, 6, 2, 7, 1):
            peer = group_peer(d)
            remote(red_t.at[peer["group"]], red_all.at[g], red_send, red_sem.at[g], peer).start()

    def send_ahead(t):
        @pl.when(g == t)
        def _():
            send_reduced()

    def forwards(t):
        return (core == t % CORES) & (y != t // CORES)

    def relays(t):
        return (core == t % CORES) & (y == (t // CORES - 1) % RINGS)

    def relayed(t):
        return (1,) if t == 1 else (1, 0)

    def forward(t, relay):
        for p in (1, 0):
            drain(fac_part(t, p), fac_sem.at[p, t])
            if relay and p in relayed(t):
                remote(
                    fac_part(t, p), fac_part(t, p), fac_fwd.at[1, p, t], fac_sem.at[p, t], y_peer(RINGS - 1)
                ).start()
            remote(fac_part(t, p), fac_part(t, p), fac_fwd.at[0, p, t], fac_sem.at[p, t], sibling).start()

    def pass_on(step):
        for t in range(1, GROUPS):
            if max(0, t - 2) == step:
                @pl.when(relays(t))
                def _():
                    forward(t, True)

        if step + 1 < GROUPS:
            @pl.when(forwards(step + 1) & jnp.logical_not(relays(step + 1)))
            def _():
                forward(step + 1, False)

    send_ahead(1)
    send_ahead(2)
    send_factors_of(1, 3, (0,))

    def spread(t, h):
        mine = gath[t][h]
        for dx, dz in OFFSETS:
            remote(mine.at[o], mine.at[o], x_send.at[t, h], x_sem.at[t, h], owner(dx, dz)).start()

    for t in range(GROUPS):
        if t == 1:
            for other in range(1, GROUPS):
                @pl.when(g != other)
                def _():
                    drain(idx_v.at[other], idx_sem.at[other])
            copy = pltpu.make_async_copy(idx_v, idx_s, idx_local)
            copy.start()
            copy.wait()
        if t:
            drain(red_all.at[t], red_sem.at[t])

            @pl.when(jnp.logical_not(forwards(t)))
            def _():
                for p in range(2):
                    drain(fac_part(t, p), fac_sem.at[p, t])

        for h in range(HALVES):
            mine = gath[t][h]
            if t == 0:
                drain(mine.at[o], first_sem.at[h])
                spread(t, h)
                continue
            before = gath[t - 1][h]
            drain(before.at[pl.ds(0, OWNERS - 1)], x_sem.at[t - 1, h])
            chosen = jnp.concatenate([before[idx_s[t, 0, k]] for k in range(SLOTS)], axis=1)
            factors = jnp.concatenate([fac_all[t, k] for k in range(SLOTS)], axis=1)
            coupling = lax.dot_general(chosen, factors, NT, preferred_element_type=F32)
            corrected = (red_all[t, pl.ds(h * HALF, HALF), :] - coupling).astype(BF16)
            solved = lax.dot_general(corrected, fac_all[t, SLOTS], NT, preferred_element_type=F32)
            mine[o] = solved.astype(BF16)
            if t < GROUPS - 1:
                spread(t, h)

            @pl.when(g == t)
            def _():
                pltpu.make_async_copy(mine.at[o], home.at[g, h], home_sem).start()

            @pl.when(g != t)
            def _():
                remote(
                    mine.at[o], home.at[g, h], home_send.at[t, h], home_sem, {"group": t}
                ).start()

        if t + 3 < GROUPS:
            send_ahead(t + 3)
            send_factors_of(t + 3, t + 4)
        if t < GROUPS - 1:
            pass_on(t)

    for c in range(LOADS):
        part = pl.ds(c * rows, rows)
        pltpu.make_async_copy(sol_v.at[part], sub_out.at[0, part], sub_sem.at[c]).wait()

    @pl.when(g >= 1)
    def _():
        drain(red_t.at[pl.ds(0, GROUPS - 1)], red_send)
        drain(idx_v.at[pl.ds(0, GROUPS - 1)], idx_send)
        for d in (0, 1, 3):
            for p in range(2):
                drain(fac_part(0, p), fac_send.at[p, d])

    @pl.when(g == 1)
    def _():
        drain(fac_part(0, 0), fac_send.at[0, 2])

    @pl.when(g == 0)
    def _():
        drain(first_t.at[pl.ds(0, GROUPS - 1)], first_send)
        for p in range(2):
            drain(fac_part(0, p), fac_sem.at[p, 0])

    for t in range(1, GROUPS):
        @pl.when(forwards(t))
        def _():
            for p in range(2):
                drain(fac_part(t, p), fac_fwd.at[0, p, t])

        @pl.when(relays(t))
        def _():
            for p in relayed(t):
                drain(fac_part(t, p), fac_fwd.at[1, p, t])

    def sent(t):
        for h in range(HALVES):
            if t < GROUPS - 1:
                drain(gath[t][h].at[pl.ds(0, OWNERS - 1)], x_send.at[t, h])
            if t:
                @pl.when(g != t)
                def _():
                    drain(gath[t][h].at[0], home_send.at[t, h])

    for t in range(GROUPS - 1):
        sent(t)
    @pl.when(g >= 1)
    def _():
        drain(home, home_sem)
        whole = home[...].reshape(COLUMNS, BLOCK).astype(F32)
        sep_out[0] = jnp.transpose(whole).astype(BF16)


    sent(GROUPS - 1)


def on_device(*args):
    dma = pltpu.SemaphoreType.DMA
    scratch = [
        pltpu.VMEM((SUBS * BLOCK, COLUMNS), BF16),
        pltpu.VMEM((SUBS, BLOCK, BLOCK), BF16),
        pltpu.VMEM((SUBS, BLOCK, BLOCK), BF16),
        pltpu.VMEM((SUBS * BLOCK, COLUMNS), BF16),
        pltpu.VMEM((BLOCK, COLUMNS), F32),
        pltpu.VMEM((BLOCK, BLOCK), BF16),
        pltpu.VMEM((GROUPS, HALVES, HALF, BLOCK), BF16),
        pltpu.VMEM((GROUPS, CHUNK, BLOCK), F32),
        pltpu.VMEM((GROUPS, CHUNK, BLOCK), F32),
        pltpu.VMEM((GROUPS, SLOTS + 1, BLOCK, BLOCK), BF16),
        pltpu.VMEM((1, SLOTS), I32),
        pltpu.SMEM((1, 1), I32),
        pltpu.VMEM((GROUPS, 1, BLOCK), I32),
        pltpu.SMEM((GROUPS, 1, BLOCK), I32),
        pltpu.VMEM((GROUPS, HALVES, HALF, BLOCK), BF16),
        *[pltpu.VMEM((OWNERS + 1, HALF, BLOCK), BF16)] * (GROUPS * HALVES),
        dma((3, LOADS)), dma((4,)), dma((LOADS,)),
        dma, dma((HALVES,)), dma, dma((GROUPS,)),
        dma((2, RINGS)), dma((2, 2, GROUPS)), dma((2, GROUPS)),
        dma, dma((GROUPS,)), dma,
        dma((GROUPS, HALVES)), dma((GROUPS, HALVES)), dma((GROUPS, HALVES)), dma,
    ]
    return pl.pallas_call(
        kernel,
        out_shape=(
            jax.ShapeDtypeStruct((1, BLOCK, COLUMNS), BF16),
            jax.ShapeDtypeStruct((1, SUBS * BLOCK, COLUMNS), BF16),
        ),
        in_specs=[pl.BlockSpec(memory_space=pl.ANY)] * 8,
        out_specs=[pl.BlockSpec(memory_space=pltpu.VMEM), pl.BlockSpec(memory_space=pl.ANY)],
        scratch_shapes=scratch,
        compiler_params=pltpu.CompilerParams(
            collective_id=0, has_side_effects=True, vmem_limit_bytes=48 << 20
        ),
    )(*[a if i == 4 else pltpu.with_memory_space_constraint(a, pltpu.HBM) for i, a in enumerate(args)])


def solution(mesh):
    rows = P("group", "blk", None)
    blocks = P("group", "blk", None, None)
    flat = P("group", "blk")
    return jax.shard_map(
        on_device,
        mesh=mesh,
        in_specs=(rows, blocks, blocks, flat, flat, rows, blocks, blocks),
        out_specs=(rows, rows),
        check_vma=False,
    )
```

```python
import jax
import jax.numpy as jnp
from jax import lax
from jax.experimental import pallas as pl
from jax.experimental.pallas import tpu as pltpu
from jax.sharding import PartitionSpec as P

MESH = pl.DeviceIdType.MESH
F32, BF16, I32 = jnp.float32, jnp.bfloat16, jnp.int32

GROUPS = 8
CORES = 2
RINGS = GROUPS // CORES
XS, ZS = 4, 8
OWNERS = XS * ZS
BLOCK = 128
COLUMNS = 256
CHUNK = COLUMNS // GROUPS
HALVES = 2
HALF = CHUNK // HALVES
SLOTS = 16
SUBS = 32
LOADS = 4
PER = SUBS // LOADS
MEET_AT = 2

PARTS = ((0, SLOTS // 2), (SLOTS // 2, SLOTS // 2))

NT = (((1,), (1,)), ((), ()))


def ring(step, size):
    return min(step, size - step)


OFFSETS = sorted(
    ((dx, dz) for dx in range(XS) for dz in range(ZS) if (dx, dz) != (0, 0)),
    key=lambda p: -(ring(p[0], XS) + ring(p[1], ZS)),
)


def kernel(
    sep_rhs, sep_inv, fac, src, count, sub_rhs, sub_inv, sub_coup,
    sep_out, sub_out,
    rhs_v, inv_v, coup_v, sol_v, sep_v, low_v, first_t, red_t, red_all, fac_all,
    src_v, count_s, idx_v, idx_s, home,
    *rest,
):
    gath = [rest[t * HALVES : (t + 1) * HALVES] for t in range(GROUPS)]
    (
        load_sem, small_sem, sub_sem, first_send, first_sem, red_send, red_sem, fac_send, fac_fwd, fac_sem,
        idx_send, idx_sem, idx_local, x_send, x_sem, home_send, home_sem,
    ) = rest[GROUPS * HALVES :]
    g, o = lax.axis_index("group"), lax.axis_index("blk")
    y, core = g // CORES, lax.rem(g, CORES)
    x, z = o // ZS, lax.rem(o, ZS)

    def owner(dx, dz):
        return {"blk": lax.rem(x + dx, XS) * ZS + lax.rem(z + dz, ZS)}

    def group_peer(d):
        return {"group": lax.rem(g + d, GROUPS)}

    def y_peer(d):
        return {"group": lax.rem(y + d, RINGS) * CORES + core}

    sibling = {"group": y * CORES + 1 - core}

    def remote(source, target, send, recv, device):
        return pltpu.make_async_remote_copy(
            src_ref=source, dst_ref=target, send_sem=send, recv_sem=recv,
            device_id=device, device_id_type=MESH,
        )

    def drain(ref, sem):
        pltpu.make_async_copy(ref, ref, sem).wait()

    barrier = pltpu.get_barrier_semaphore()
    for dx, dz in OFFSETS:
        pl.semaphore_signal(barrier, inc=1, device_id=owner(dx, dz), device_id_type=MESH)
    for d in range(1, GROUPS):
        pl.semaphore_signal(barrier, inc=1, device_id=group_peer(d), device_id_type=MESH)

    rows = PER * BLOCK

    def loads(c):
        part, blocks = pl.ds(c * rows, rows), pl.ds(c * PER, PER)
        return (
            pltpu.make_async_copy(sub_rhs.at[0, part], rhs_v.at[part], load_sem.at[0, c]),
            pltpu.make_async_copy(sub_inv.at[0, blocks], inv_v.at[blocks], load_sem.at[1, c]),
            pltpu.make_async_copy(sub_coup.at[0, blocks], coup_v.at[blocks], load_sem.at[2, c]),
        )

    for c in range(LOADS):
        for copy in loads(c):
            copy.start()
    small = (
        pltpu.make_async_copy(sep_rhs.at[0], sep_v, small_sem.at[0]),
        pltpu.make_async_copy(src, src_v, small_sem.at[1]),
        pltpu.make_async_copy(count, count_s, small_sem.at[2]),
        pltpu.make_async_copy(sep_inv.at[0, 0], low_v, small_sem.at[3]),
    )
    for copy in small:
        copy.start()
    def pieces(p):
        first, size = PARTS[p]
        some = pl.ds(first, size)
        two = [(fac.at[0, some], fac_all.at[g, some])]
        return two + [(sep_inv.at[0, 0], fac_all.at[g, SLOTS])] * p

    def fac_part(t, p):
        first, size = PARTS[p]
        return fac_all.at[t, pl.ds(first, size + p)]

    for p in range(2):
        for source, target in pieces(p):
            pltpu.make_async_copy(source, target, fac_sem.at[p, g]).start()

    for t in range(GROUPS - 1):
        for h in range(HALVES):
            gath[t][h][OWNERS] = jnp.zeros((HALF, BLOCK), BF16)
    for copy in small:
        copy.wait()
    slot = lax.broadcasted_iota(I32, (1, SLOTS), 1)
    idx_v[0] = jnp.zeros((1, BLOCK), I32)
    idx_v[g] = jnp.zeros((1, BLOCK), I32)
    idx_v[g, :, pl.ds(0, SLOTS)] = jnp.where(slot < count_s[0, 0], src_v[...], OWNERS)

    def send_factors(parts=(1, 0)):
        def to(d, p):
            for source, target in pieces(p):
                peer = y_peer(d) if d else sibling
                remote(source, target, fac_send.at[p, d], fac_sem.at[p, g], peer).start()

        if 1 in parts:
            to(3, 1)
            to(1, 1)

        if 0 in parts:
            @pl.when(g == 1)
            def _():
                to(2, 0)

            to(3, 0)
            to(1, 0)
            to(0, 1)
            to(0, 0)

    def send_factors_of(t, until, parts=(1, 0)):
        @pl.when((g >= t) & (g < until))
        def _():
            send_factors(parts)

    def send_indices():
        for d in range(1, GROUPS):
            remote(idx_v.at[g], idx_v.at[g], idx_send, idx_sem.at[g], group_peer(d)).start()

    def solve(c):
        for copy in loads(c):
            copy.wait()
        for i in range(PER):
            n = c * PER + i
            own = pl.ds(pl.multiple_of(n * BLOCK, BLOCK), BLOCK)
            sol = jnp.dot(inv_v[n], rhs_v[own, :], preferred_element_type=F32)
            sol_v[own, :] = sol.astype(BF16)
        part = pl.ds(pl.multiple_of(c * rows, rows), rows)
        pltpu.make_async_copy(sol_v.at[part], sub_out.at[0, part], sub_sem.at[c]).start()

    def lift(c, total):
        part = pl.ds(pl.multiple_of(c * rows, rows), rows)
        coup = jnp.concatenate([coup_v[c * PER + i] for i in range(PER)], axis=1)
        return total + jnp.dot(coup, sol_v[part, :], preferred_element_type=F32)

    def subtree(c, total):
        total = lift(c - 1, total)
        solve(c)
        return total

    solve(0)
    lifted = lax.fori_loop(1, MEET_AT, subtree, jnp.zeros((BLOCK, COLUMNS), F32))

    pl.semaphore_wait(barrier, len(OFFSETS) + GROUPS - 1)
    @pl.when(g >= 1)
    def _():
        send_indices()

    send_factors_of(1, 3, (1,))
    send_factors_of(1, 2, (0,))

    lifted = lax.fori_loop(MEET_AT, LOADS, subtree, lifted)
    lifted = lift(LOADS - 1, lifted)
    reduced = sep_v[...] - lifted
    red_t[...] = jnp.transpose(reduced).reshape(GROUPS, CHUNK, BLOCK)
    @pl.when(g == 0)
    def _():
        first = jnp.dot(low_v[...], reduced.astype(BF16), preferred_element_type=F32)
        first_t[...] = jnp.transpose(first).astype(BF16).reshape(GROUPS, HALVES, HALF, BLOCK)
        sep_out[0] = first.astype(BF16)

    @pl.when(g == 0)
    def _():
        for h in range(HALVES):
            for d in (4, 5, 3, 2, 6, 7, 1):
                remote(
                    first_t.at[d, h], gath[0][h].at[o], first_send, first_sem.at[h], {"group": d}
                ).start()
            pltpu.make_async_copy(first_t.at[0, h], gath[0][h].at[o], first_sem.at[h]).start()

    def send_reduced():
        pltpu.make_async_copy(red_t.at[g], red_all.at[g], red_sem.at[g]).start()
        for d in (4, 5, 3, 6, 2, 7, 1):
            peer = group_peer(d)
            remote(red_t.at[peer["group"]], red_all.at[g], red_send, red_sem.at[g], peer).start()

    def send_ahead(t):
        @pl.when(g == t)
        def _():
            send_reduced()

    def forwards(t):
        return (core == t % CORES) & (y != t // CORES)

    def relays(t):
        return (core == t % CORES) & (y == (t // CORES - 1) % RINGS)

    def relayed(t):
        return (1,) if t == 1 else (1, 0)

    def forward(t, relay):
        for p in (1, 0):
            drain(fac_part(t, p), fac_sem.at[p, t])
            if relay and p in relayed(t):
                remote(
                    fac_part(t, p), fac_part(t, p), fac_fwd.at[1, p, t], fac_sem.at[p, t], y_peer(RINGS - 1)
                ).start()
            remote(fac_part(t, p), fac_part(t, p), fac_fwd.at[0, p, t], fac_sem.at[p, t], sibling).start()

    def pass_on(step):
        for t in range(1, GROUPS):
            if max(0, t - 2) == step:
                @pl.when(relays(t))
                def _():
                    forward(t, True)

        if step + 1 < GROUPS:
            @pl.when(forwards(step + 1) & jnp.logical_not(relays(step + 1)))
            def _():
                forward(step + 1, False)

    send_ahead(1)
    send_ahead(2)
    send_factors_of(2, 3, (0,))

    def spread(t, h):
        mine = gath[t][h]
        for dx, dz in OFFSETS:
            remote(mine.at[o], mine.at[o], x_send.at[t, h], x_sem.at[t, h], owner(dx, dz)).start()

    for t in range(GROUPS):
        if t == 1:
            for other in range(1, GROUPS):
                @pl.when(g != other)
                def _():
                    drain(idx_v.at[other], idx_sem.at[other])
            copy = pltpu.make_async_copy(idx_v, idx_s, idx_local)
            copy.start()
            copy.wait()
        if t:
            drain(red_all.at[t], red_sem.at[t])

            @pl.when(jnp.logical_not(forwards(t)))
            def _():
                for p in range(2):
                    drain(fac_part(t, p), fac_sem.at[p, t])

        for h in range(HALVES):
            mine = gath[t][h]
            if t == 0:
                drain(mine.at[o], first_sem.at[h])
                spread(t, h)
                continue
            before = gath[t - 1][h]
            drain(before.at[pl.ds(0, OWNERS - 1)], x_sem.at[t - 1, h])
            chosen = jnp.concatenate([before[idx_s[t, 0, k]] for k in range(SLOTS)], axis=1)
            factors = jnp.concatenate([fac_all[t, k] for k in range(SLOTS)], axis=1)
            coupling = lax.dot_general(chosen, factors, NT, preferred_element_type=F32)
            corrected = (red_all[t, pl.ds(h * HALF, HALF), :] - coupling).astype(BF16)
            solved = lax.dot_general(corrected, fac_all[t, SLOTS], NT, preferred_element_type=F32)
            mine[o] = solved.astype(BF16)
            if t < GROUPS - 1:
                spread(t, h)

            @pl.when(g == t)
            def _():
                pltpu.make_async_copy(mine.at[o], home.at[g, h], home_sem).start()

            @pl.when(g != t)
            def _():
                remote(
                    mine.at[o], home.at[g, h], home_send.at[t, h], home_sem, {"group": t}
                ).start()

        if t + 3 < GROUPS:
            send_ahead(t + 3)
            send_factors_of(t + 3, t + 4)
        if t < GROUPS - 1:
            pass_on(t)

    for c in range(LOADS):
        part = pl.ds(c * rows, rows)
        pltpu.make_async_copy(sol_v.at[part], sub_out.at[0, part], sub_sem.at[c]).wait()

    @pl.when(g >= 1)
    def _():
        drain(red_t.at[pl.ds(0, GROUPS - 1)], red_send)
        drain(idx_v.at[pl.ds(0, GROUPS - 1)], idx_send)
        for d in (0, 1, 3):
            for p in range(2):
                drain(fac_part(0, p), fac_send.at[p, d])

    @pl.when(g == 1)
    def _():
        drain(fac_part(0, 0), fac_send.at[0, 2])

    @pl.when(g == 0)
    def _():
        drain(first_t.at[pl.ds(0, GROUPS - 1)], first_send)
        for p in range(2):
            drain(fac_part(0, p), fac_sem.at[p, 0])

    for t in range(1, GROUPS):
        @pl.when(forwards(t))
        def _():
            for p in range(2):
                drain(fac_part(t, p), fac_fwd.at[0, p, t])

        @pl.when(relays(t))
        def _():
            for p in relayed(t):
                drain(fac_part(t, p), fac_fwd.at[1, p, t])

    def sent(t):
        for h in range(HALVES):
            if t < GROUPS - 1:
                drain(gath[t][h].at[pl.ds(0, OWNERS - 1)], x_send.at[t, h])
            if t:
                @pl.when(g != t)
                def _():
                    drain(gath[t][h].at[0], home_send.at[t, h])

    for t in range(GROUPS - 1):
        sent(t)
    @pl.when(g >= 1)
    def _():
        drain(home, home_sem)
        whole = home[...].reshape(COLUMNS, BLOCK).astype(F32)
        sep_out[0] = jnp.transpose(whole).astype(BF16)


    sent(GROUPS - 1)


def on_device(*args):
    dma = pltpu.SemaphoreType.DMA
    scratch = [
        pltpu.VMEM((SUBS * BLOCK, COLUMNS), BF16),
        pltpu.VMEM((SUBS, BLOCK, BLOCK), BF16),
        pltpu.VMEM((SUBS, BLOCK, BLOCK), BF16),
        pltpu.VMEM((SUBS * BLOCK, COLUMNS), BF16),
        pltpu.VMEM((BLOCK, COLUMNS), F32),
        pltpu.VMEM((BLOCK, BLOCK), BF16),
        pltpu.VMEM((GROUPS, HALVES, HALF, BLOCK), BF16),
        pltpu.VMEM((GROUPS, CHUNK, BLOCK), F32),
        pltpu.VMEM((GROUPS, CHUNK, BLOCK), F32),
        pltpu.VMEM((GROUPS, SLOTS + 1, BLOCK, BLOCK), BF16),
        pltpu.VMEM((1, SLOTS), I32),
        pltpu.SMEM((1, 1), I32),
        pltpu.VMEM((GROUPS, 1, BLOCK), I32),
        pltpu.SMEM((GROUPS, 1, BLOCK), I32),
        pltpu.VMEM((GROUPS, HALVES, HALF, BLOCK), BF16),
        *[pltpu.VMEM((OWNERS + 1, HALF, BLOCK), BF16)] * (GROUPS * HALVES),
        dma((3, LOADS)), dma((4,)), dma((LOADS,)),
        dma, dma((HALVES,)), dma, dma((GROUPS,)),
        dma((2, RINGS)), dma((2, 2, GROUPS)), dma((2, GROUPS)),
        dma, dma((GROUPS,)), dma,
        dma((GROUPS, HALVES)), dma((GROUPS, HALVES)), dma((GROUPS, HALVES)), dma,
    ]
    return pl.pallas_call(
        kernel,
        out_shape=(
            jax.ShapeDtypeStruct((1, BLOCK, COLUMNS), BF16),
            jax.ShapeDtypeStruct((1, SUBS * BLOCK, COLUMNS), BF16),
        ),
        in_specs=[pl.BlockSpec(memory_space=pl.ANY)] * 8,
        out_specs=[pl.BlockSpec(memory_space=pltpu.VMEM), pl.BlockSpec(memory_space=pl.ANY)],
        scratch_shapes=scratch,
        compiler_params=pltpu.CompilerParams(
            collective_id=0, has_side_effects=True, vmem_limit_bytes=48 << 20
        ),
    )(*[a if i == 4 else pltpu.with_memory_space_constraint(a, pltpu.HBM) for i, a in enumerate(args)])


def solution(mesh):
    rows = P("group", "blk", None)
    blocks = P("group", "blk", None, None)
    flat = P("group", "blk")
    return jax.shard_map(
        on_device,
        mesh=mesh,
        in_specs=(rows, blocks, blocks, flat, flat, rows, blocks, blocks),
        out_specs=(rows, rows),
        check_vma=False,
    )
```
